256 devices in a mesh: guide: 2 (over core), seq: 128 (over x, z, y).
Axes of the slice: x: 4, y: 4, z: 8, core: 2. Of those that a mesh axis runs over, the one named last changes fastest.
Arguments:
- hidden: bfloat16 [2, 24576, 3072], P('guide', 'seq'), may hold values from -6 to 6
- query_rows: bfloat16 [2, 24576, 1536], P('guide', 'seq'), may hold values from -6 to 6
- key_rows: bfloat16 [2, 24576, 1536], P('guide', 'seq'), may hold values from -6 to 6
- value_rows: bfloat16 [2, 24576, 1536], P('guide', 'seq'), may hold values from -6 to 6
- text_lengths: int32 [2, 32], P('guide'), may hold values from 1 to 512, as said below
- q_gain: float32 [128], replicated, may hold values from 0.6 to 6
- k_gain: float32 [128], replicated, may hold values from 0.6 to 6
- o_weight: bfloat16 [1536, 3072], P('guide'), may hold values from -0.15625 to 0.15625
- layer_gate: float32 [2, 32, 3072], P('guide'), may hold values from -5 to 5
- final_shift: float32 [2, 32, 3072], P('guide'), may hold values from -3 to 3
- final_scale: float32 [2, 32, 3072], P('guide'), may hold values from -2.5 to 2.5
- final_weight: bfloat16 [3072, 64], replicated, may hold values from -0.109375 to 0.109375
- final_bias: float32 [64], replicated, may hold values from -3 to 3
- latents: float32 [8192, 64], P('seq', 'guide'), may hold values from -6 to 6
- step_delta: float32 [32], replicated, may hold values from -0.6 to -0.2
Outputs:
- new_latents: float32 [8192, 64], P('seq', 'guide')
- hidden_out: bfloat16 [2, 24576, 3072], P('guide', 'seq')
- hidden_rms: float32 [2, 32], P('guide')
- hidden_peak: float32 [2, 32], P('guide')
The draws below stay inside these ranges and needn't reach their ends.
Inputs may be any that keep to these rules, and one draw needn't show every extreme that they name: `text_lengths`: some request of some half has all 512 text slots live.
All inputs are finite; a program needn't handle non-finite values.
Results may differ from the reference program's by a relative error of at most 0.015.
The reference program's roundings to bfloat16 on the way (of `queries_normed`, `keys_normed`, `weights`, `attended` and `modulated`) count: a program that leaves them out, or rounds other values in their place, can miss the bound.
Values may be sent and summed in bfloat16 or wider, within the bound.
A program may use at most 128 MiB of HBM per device.

```python
import math
import jax
import jax.numpy as jnp
from jax import lax

D = 3072
HEADS = 12
HD = 128
OUT_CH = 64
TXT = 512
GROUP = 4
IMG = 256
TXT_DEV = 128
IMG_DEV = 64
BLOCK = 192
REQS = 32
TOKENS = 24576
LATENT_ROWS = 8192
N_GUIDE = 2


def paired_rows(key):
    full_shape = (N_GUIDE, TOKENS, HEADS * HD)
    keys_base = jax.random.normal(jax.random.fold_in(key, 21), full_shape, jnp.float32)
    query_base = jax.random.normal(jax.random.fold_in(key, 22), full_shape, jnp.float32)
    return (jnp.clip(query_base, -6.0, 6.0), jnp.clip(keys_base, -6.0, 6.0))


def draw_query_rows(key, part):
    return paired_rows(key)[0].astype(jnp.bfloat16)


def draw_key_rows(key, part):
    return paired_rows(key)[1].astype(jnp.bfloat16)


def gain_values(key):
    return jax.random.uniform(key, (HD,), jnp.float32, 0.6, 1.8)


def draw_q_gain(key, part):
    return gain_values(jax.random.fold_in(key, 31))


def draw_k_gain(key, part):
    return gain_values(jax.random.fold_in(key, 32))


def draw_text_lengths(key, part):
    values = jax.random.randint(jax.random.fold_in(key, 41), (N_GUIDE * REQS,), 1, TXT + 1)
    forced = jax.random.randint(jax.random.fold_in(key, 42), (), 0, N_GUIDE * REQS)
    values = values.at[forced].set(TXT)
    return values.reshape(N_GUIDE, REQS).astype(jnp.int32)


def shard_levels(own_key, shape, cuts, low, high):
    def one(axis_at, blocks):
        draws = jax.random.uniform(jax.random.fold_in(jax.random.fold_in(own_key, 6), axis_at), (blocks,), jnp.float32, low / len(cuts), high / len(cuts))
        return jnp.repeat(jnp.exp(draws), shape[axis_at] // blocks).reshape((-1,) + (1,) * (len(shape) - axis_at - 1))

    factor_of = one(*cuts[0])
    for cut in cuts[1:]:
        factor_of = factor_of * one(*cut)
    return factor_of


def centred(stream_key, shape, deviation, limit, split=(), kind=jnp.bfloat16):
    values = jax.random.normal(stream_key, shape, jnp.float32) * deviation
    if len(split) > 0:
        values = shard_levels(stream_key, shape, split, -0.22, 0.18) * values
    return jnp.clip(values, min=-limit, max=limit).astype(kind)


def setup_inputs(seed: int = 0) -> dict:
    streams_of = jax.random.split(jax.random.key(seed), 16)
    return {
        "hidden": centred(streams_of[0], (N_GUIDE, TOKENS, D), 1.0, 6.0, ((0, 2), (1, 128))),
        "query_rows": draw_query_rows(jax.random.fold_in(streams_of[15], 71), 0),
        "key_rows": draw_key_rows(jax.random.fold_in(streams_of[15], 71), 0),
        "value_rows": centred(streams_of[3], (N_GUIDE, TOKENS, HEADS * HD), 1.0, 6.0, ((0, 2), (1, 128))),
        "text_lengths": draw_text_lengths(jax.random.fold_in(streams_of[15], 71), 0),
        "q_gain": draw_q_gain(jax.random.fold_in(streams_of[15], 71), 0),
        "k_gain": draw_k_gain(jax.random.fold_in(streams_of[15], 71), 0),
        "o_weight": centred(streams_of[7], (HEADS * HD, D), (HEADS * HD) ** -0.5, 0.15625, ((0, 2),)),
        "layer_gate": centred(streams_of[8], (N_GUIDE, REQS, D), 1.0, 5.0, ((0, 2),), jnp.float32),
        "final_shift": centred(streams_of[9], (N_GUIDE, REQS, D), 0.5, 3.0, ((0, 2),), jnp.float32),
        "final_scale": centred(streams_of[10], (N_GUIDE, REQS, D), 0.3, 2.5, ((0, 2),), jnp.float32),
        "final_weight": centred(streams_of[11], (D, OUT_CH), D ** -0.5, 0.109375),
        "final_bias": centred(streams_of[12], (OUT_CH,), 0.5, 3.0, (), jnp.float32),
        "latents": centred(streams_of[13], (LATENT_ROWS, OUT_CH), 1.0, 6.0, ((0, 128), (1, 2)), jnp.float32),
        "step_delta": jnp.clip(jax.random.uniform(streams_of[14], (REQS,), jnp.float32, -0.6, -0.2), -0.6, -0.2),
    }


guidance_weight = 3.5

def normalize_heads(raw_rows, channel_gain, factor):
    values = raw_rows.astype(jnp.float32)
    inv_rms = lax.rsqrt(lax.optimization_barrier(jnp.mean(values * values, axis=-1, keepdims=True)) + 1e-06)
    return (values * inv_rms * channel_gain * factor).astype(jnp.bfloat16)

def to_requests(array):
    last = array.shape[-1]
    blocks = array.reshape(N_GUIDE, GROUP, REQS, BLOCK, last).transpose(0, 2, 1, 3, 4)
    return blocks.reshape(N_GUIDE * REQS, GROUP * BLOCK, last)

def reference(hidden, query_rows, key_rows, value_rows, text_lengths, q_gain, k_gain, o_weight, layer_gate, final_shift, final_scale, final_weight, final_bias, latents, step_delta):
    seq_len = GROUP * BLOCK
    count = N_GUIDE * REQS

    def one_request(request_item):
        hid, qry, kys, vls, length, gate_row, shift_row, scale_row = request_item
        queries_normed = normalize_heads(qry.reshape(seq_len, HEADS, HD), q_gain, 1.0 / math.sqrt(HD))
        keys_normed = normalize_heads(kys.reshape(seq_len, HEADS, HD), k_gain, 1.0)
        values = vls.reshape(seq_len, HEADS, HD)
        position = jnp.arange(seq_len, dtype=jnp.int32)
        within = position % BLOCK
        block_index = position // BLOCK
        usable = (within >= TXT_DEV) | (block_index * TXT_DEV + within < length)
        scores = jnp.einsum('qhd,khd->hqk', queries_normed.astype(jnp.float32), keys_normed.astype(jnp.float32))
        scores = jnp.where(usable[None, None, :], scores, jnp.float32(-1e+30))
        running_max = lax.optimization_barrier(jnp.max(scores, axis=-1, keepdims=True))
        weights = jnp.exp(scores - running_max)
        weights = (weights / lax.optimization_barrier(jnp.sum(weights, axis=-1, keepdims=True))).astype(jnp.bfloat16)
        attended = jnp.einsum('hqk,khd->qhd', weights.astype(jnp.float32), values.astype(jnp.float32))
        attended = attended.reshape(seq_len, HEADS * HD).astype(jnp.bfloat16)
        projected = jnp.dot(attended, o_weight, preferred_element_type=jnp.float32)
        hidden_new = (hid.astype(jnp.float32) + gate_row[None, :] * projected).astype(jnp.bfloat16)
        widened = hidden_new.astype(jnp.float32)
        square_sum = jnp.sum(widened * widened)
        peak_abs = jnp.max(jnp.abs(widened))
        image_rows = widened.reshape(GROUP, BLOCK, D)[:, TXT_DEV:, :].reshape(IMG, D)
        row_mean = lax.optimization_barrier(jnp.mean(image_rows, axis=-1, keepdims=True))
        centered = image_rows - row_mean
        row_var = lax.optimization_barrier(jnp.mean(centered * centered, axis=-1, keepdims=True))
        normed = centered * lax.rsqrt(row_var + 1e-06)
        modulated = (normed * (1.0 + scale_row[None, :]) + shift_row[None, :]).astype(jnp.bfloat16)
        velocity = jnp.dot(modulated, final_weight, preferred_element_type=jnp.float32) + final_bias[None, :]
        return (hidden_new, square_sum, peak_abs, velocity)
    request_items = (to_requests(hidden), to_requests(query_rows), to_requests(key_rows), to_requests(value_rows), text_lengths.reshape(count), layer_gate.reshape(count, D), final_shift.reshape(count, D), final_scale.reshape(count, D))
    hidden_new, square_sum, peak_abs, velocity = lax.map(one_request, request_items)
    hidden_out = hidden_new.reshape(N_GUIDE, REQS, GROUP, BLOCK, D).transpose(0, 2, 1, 3, 4).reshape(N_GUIDE, TOKENS, D)
    hidden_rms = jnp.sqrt(square_sum.reshape(N_GUIDE, REQS) / (GROUP * BLOCK * D) + 1e-06)
    hidden_peak = peak_abs.reshape(N_GUIDE, REQS)
    velocity = velocity.reshape(N_GUIDE, REQS, IMG, OUT_CH)
    conditional = velocity[0]
    unconditional = velocity[1]
    guided = unconditional + guidance_weight * (conditional - unconditional)
    ordered = latents.reshape(GROUP, REQS, IMG_DEV, OUT_CH).transpose(1, 0, 2, 3).reshape(REQS, IMG, OUT_CH)
    new_latents = ordered + step_delta[:, None, None] * guided
    new_latents = new_latents.reshape(REQS, GROUP, IMG_DEV, OUT_CH).transpose(1, 0, 2, 3)
    return (new_latents.reshape(LATENT_ROWS, OUT_CH), hidden_out, hidden_rms, hidden_peak)
```

```python
import functools
import math

import jax
import jax.numpy as jnp
from jax import lax
from jax.experimental import pallas as pl
from jax.experimental.pallas import tpu as pltpu
from jax.sharding import PartitionSpec as P

HD = 128
GROUP = 4
TXT_DEV = 128
IMG_DEV = 64
BLOCK = TXT_DEV + IMG_DEV
HPD = 3
GUIDANCE = 3.5
ORDER = (2, 1, 3)


def normalize(rows, gain, factor):
    values = rows.astype(jnp.float32)
    inv = lax.rsqrt(jnp.mean(values * values, axis=-1, keepdims=True) + 1e-06)
    return (values * inv * gain * factor).astype(jnp.bfloat16)


def kernel(
    reqs,
    y_size,
    chunk,
    hidden,
    query,
    key,
    value,
    lengths,
    q_gain,
    k_gain,
    o_weight,
    gate,
    shift,
    scale,
    f_weight,
    f_bias,
    latents,
    delta,
    new_latents,
    hidden_out,
    rms_out,
    peak_out,
    qb,
    kb,
    vb,
    ob,
    att,
    wb,
    hid,
    outb,
    part,
    gate_b,
    shift_b,
    scale_b,
    fw_b,
    bias_b,
    lat_b,
    len_b,
    delta_b,
    qg_b,
    kg_b,
    vel_own,
    vel_got,
    st_x,
    st_y,
    st_z,
    in_send,
    in_recv,
    in_local,
    o_send,
    o_recv,
    w_send,
    w_recv,
    w_local,
    loc,
    out_sem,
    v_sem,
    s_send,
    s_recv,
):
    z_size = reqs // y_size
    width = hidden.shape[2]
    heads = GROUP * HPD
    g = lax.axis_index("guide")
    s = lax.axis_index("seq")
    x = s // reqs
    r = s % reqs
    y = r % y_size
    z = r // y_size

    def seq_of(xx, zz, yy):
        return xx * reqs + zz * y_size + yy

    def x_peer(o):
        return lax.rem(x + o, GROUP)

    def y_peer(o):
        return seq_of(x, z, lax.rem(y + o, y_size))

    def z_peer(o):
        return seq_of(x, lax.rem(z + o, z_size), y)

    tensors = ((key, kb), (value, vb), (query, qb))

    def columns(owner, h):
        return pl.ds(pl.multiple_of((owner * HPD + h) * HD, HD), HD)

    own = []
    for h in range(HPD):
        row = []
        for i, (src, dst) in enumerate(tensors):
            c = pltpu.make_async_copy(
                src.at[0, :, columns(x, h)], dst.at[h, x], in_local.at[i, h]
            )
            c.start()
            row.append(c)
        own.append(row)
    group8 = pl.ds(pl.multiple_of((r // 8) * 8, 8), 8) if reqs >= 8 else pl.ds(0, reqs)
    row8 = r % 8
    small = [
        (q_gain, qg_b),
        (k_gain, kg_b),
        (lengths, len_b),
        (gate.at[0, group8], gate_b),
        (hidden.at[0], hid),
        (shift.at[0, group8], shift_b),
        (scale.at[0, group8], scale_b),
        (f_weight, fw_b),
        (f_bias, bias_b),
        (latents, lat_b),
        (delta, delta_b),
    ]
    small = [pltpu.make_async_copy(a, b, loc.at[i]) for i, (a, b) in enumerate(small)]
    for c in small:
        c.start()

    barrier = pltpu.get_barrier_semaphore()
    for o in range(1, GROUP):
        pl.semaphore_signal(barrier, inc=1, device_id={"seq": seq_of(x_peer(o), z, y)})
    pl.semaphore_signal(barrier, inc=1, device_id={"guide": 1 - g})
    for o in range(1, y_size):
        pl.semaphore_signal(barrier, inc=1, device_id={"seq": y_peer(o)})
    for o in range(1, z_size):
        pl.semaphore_signal(barrier, inc=1, device_id={"seq": z_peer(o)})
    pl.semaphore_wait(barrier, GROUP + y_size - 1 + z_size - 1)

    def exchange(i, h, o):
        src, dst = tensors[i]
        t = x_peer(o)
        return pltpu.make_async_remote_copy(
            src_ref=src.at[0, :, columns(t, h)],
            dst_ref=dst.at[h, x],
            send_sem=in_send.at[i, h, o - 1],
            recv_sem=in_recv.at[i, h, o - 1],
            device_id={"seq": seq_of(t, z, y)},
        )

    for h in range(HPD):
        for i in range(3):
            for o in ORDER:
                exchange(i, h, o).start()

    def weight_pieces():
        first = (HPD - 1) * HD
        pieces = []
        for p in range(GROUP // 2):
            owner = g * (GROUP // 2) + p
            pieces.append((pl.ds(p * HPD * HD, first), pl.ds(pl.multiple_of(owner * first, HD), first)))
            pieces.append(
                (
                    pl.ds(p * HPD * HD + first, HD),
                    pl.ds(pl.multiple_of(GROUP * first + owner * HD, HD), HD),
                )
            )
        return pieces

    weight_sends, weight_locals = [], []
    for i, (a, b) in enumerate(weight_pieces()):
        c = pltpu.make_async_remote_copy(
            src_ref=o_weight.at[a],
            dst_ref=wb.at[b],
            send_sem=w_send.at[i],
            recv_sem=w_recv.at[i],
            device_id={"guide": 1 - g},
        )
        c.start()
        weight_sends.append(c)
        c = pltpu.make_async_copy(o_weight.at[a], wb.at[b], w_local.at[i])
        c.start()
        weight_locals.append(c)

    def give_back(h, o):
        t = x_peer(o)
        return pltpu.make_async_remote_copy(
            src_ref=ob.at[h, t],
            dst_ref=att.at[x * HPD + h],
            send_sem=o_send.at[h, o - 1],
            recv_sem=o_recv.at[h, o - 1],
            device_id={"seq": seq_of(t, z, y)},
        )

    for c in small[:3]:
        c.wait()
    lane = lax.broadcasted_iota(jnp.int32, (1, len_b.shape[1]), 1)
    length = jnp.sum(jnp.where(lane == r, len_b[...], 0), axis=1, keepdims=True)
    position = lax.broadcasted_iota(jnp.int32, (1, GROUP * BLOCK), 1)
    within = position % BLOCK
    usable = (within >= TXT_DEV) | ((position // BLOCK) * TXT_DEV + within < length)
    bias = jnp.where(usable, 0.0, -1e30).astype(jnp.float32)
    q_gain_row = qg_b[...]
    k_gain_row = kg_b[...]
    ones = jnp.ones((GROUP * BLOCK, HD), jnp.bfloat16)

    for h in range(HPD):
        for i in range(3):
            own[h][i].wait()
            for o in ORDER:
                exchange(i, h, o).wait_recv()
        keys = normalize(kb[h].reshape(GROUP * BLOCK, HD), k_gain_row, 1.0)
        values = jnp.concatenate([vb[h].reshape(GROUP * BLOCK, HD), ones], axis=1)
        for o in ORDER + (0,):
            t = x_peer(o)
            queries = normalize(qb[h, t], q_gain_row, 1.0 / math.sqrt(HD))
            scores = lax.dot_general(
                queries, keys, (((1,), (1,)), ((), ())), preferred_element_type=jnp.float32
            )
            scores = scores + bias
            top = jnp.max(scores, axis=1, keepdims=True)
            weights = jnp.exp(scores - top).astype(jnp.bfloat16)
            both = jnp.dot(weights, values, preferred_element_type=jnp.float32)
            result = (both[:, :HD] / both[:, HD:]).astype(jnp.bfloat16)
            if o == 0:
                att[x * HPD + h] = result
            else:
                ob[h, t] = result
                give_back(h, o).start()

    for c in weight_locals:
        c.wait()
    for c in weight_sends:
        c.wait_recv()
    for h in range(HPD - 1):
        for o in ORDER:
            give_back(h, o).wait_recv()
    depth = GROUP * (HPD - 1) * HD
    first = jnp.concatenate(
        [att[p * HPD + h] for p in range(GROUP) for h in range(HPD - 1)], axis=1
    )

    def first_part(n, carry):
        cols = pl.ds(pl.multiple_of(n * chunk, chunk), chunk)
        part[:, cols] = jnp.dot(first, wb[:depth, cols], preferred_element_type=jnp.float32)
        return carry

    lax.fori_loop(0, width // chunk, first_part, 0)

    for c in small[3:]:
        c.wait()
    for o in ORDER:
        give_back(HPD - 1, o).wait_recv()
    last = jnp.concatenate([att[p * HPD + HPD - 1] for p in range(GROUP)], axis=1)

    def out_copy(n):
        cols = pl.ds(pl.multiple_of(n * chunk, chunk), chunk)
        return pltpu.make_async_copy(outb.at[:, cols], hidden_out.at[0, :, cols], out_sem.at[n])

    def last_part(n, carry):
        squares, peaks, sums = carry
        cols = pl.ds(pl.multiple_of(n * chunk, chunk), chunk)
        projected = part[:, cols] + jnp.dot(
            last, wb[depth:, cols], preferred_element_type=jnp.float32
        )
        new = (hid[:, cols].astype(jnp.float32) + gate_b[pl.ds(row8, 1), cols] * projected).astype(
            jnp.bfloat16
        )
        outb[:, cols] = new
        out_copy(n).start()
        wide = new.astype(jnp.float32)
        folded = wide.reshape(BLOCK // 8, 8, chunk)
        squares = squares + jnp.sum(folded * folded, axis=0)
        peaks = jnp.maximum(peaks, jnp.max(jnp.abs(folded), axis=0))
        part_sums = wide[TXT_DEV:]
        part[TXT_DEV:, cols] = part_sums
        for k in range(chunk // 128):
            sums = sums + part_sums[:, k * 128 : (k + 1) * 128]
        return squares, peaks, sums

    zero = jnp.zeros((8, chunk), jnp.float32)
    squares, peaks, sums = lax.fori_loop(
        0, width // chunk, last_part, (zero, zero, jnp.zeros((IMG_DEV, 128), jnp.float32))
    )

    total = jnp.sum(jnp.sum(squares, axis=1, keepdims=True), axis=0, keepdims=True)
    peak = jnp.max(jnp.max(peaks, axis=1, keepdims=True), axis=0, keepdims=True)
    sub8 = lax.broadcasted_iota(jnp.int32, (8, 128), 0)
    lane8 = lax.broadcasted_iota(jnp.int32, (8, 128), 1)

    def stage(ref, slot, base, peers):
        copies = []
        for i, peer in enumerate(peers):
            c = pltpu.make_async_remote_copy(
                src_ref=ref.at[slot],
                dst_ref=ref.at[slot],
                send_sem=s_send.at[base + i],
                recv_sem=s_recv.at[base + i],
                device_id={"seq": peer},
            )
            c.start()
            copies.append(c)
        return copies

    st_x[x] = jnp.where(sub8 == 0, total, peak)
    x_copies = stage(st_x, x, 0, [seq_of(x_peer(o), z, y) for o in range(1, GROUP)])

    mean = jnp.sum(sums, axis=1, keepdims=True) * (1.0 / width)

    def variance(n, acc):
        cols = pl.ds(pl.multiple_of(n * chunk, chunk), chunk)
        centered = part[TXT_DEV:, cols] - mean
        centered = centered * centered
        for k in range(chunk // 128):
            acc = acc + centered[:, k * 128 : (k + 1) * 128]
        return acc

    var = lax.fori_loop(0, width // chunk, variance, jnp.zeros((IMG_DEV, 128), jnp.float32))
    inv = lax.rsqrt(jnp.sum(var, axis=1, keepdims=True) * (1.0 / width) + 1e-06)

    def velocity_part(n, acc):
        cols = pl.ds(pl.multiple_of(n * chunk, chunk), chunk)
        normed = (part[TXT_DEV:, cols] - mean) * inv
        mod = (
            normed * (1.0 + scale_b[pl.ds(row8, 1), cols]) + shift_b[pl.ds(row8, 1), cols]
        ).astype(jnp.bfloat16)
        return acc + jnp.dot(mod, fw_b[cols, :], preferred_element_type=jnp.float32)

    channels = fw_b.shape[1]
    velocity = lax.fori_loop(
        0, width // chunk, velocity_part, jnp.zeros((IMG_DEV, channels), jnp.float32)
    )
    velocity = velocity + bias_b[...]
    vel_own[...] = jnp.concatenate(
        [velocity, jnp.zeros((IMG_DEV, 128 - channels), jnp.float32)], axis=1
    )
    vel_copy = pltpu.make_async_remote_copy(
        src_ref=vel_own,
        dst_ref=vel_got,
        send_sem=v_sem.at[0],
        recv_sem=v_sem.at[1],
        device_id={"guide": 1 - g},
    )
    vel_copy.start()

    for c in x_copies:
        c.wait_recv()
    added, largest = st_x[0], st_x[0]
    for i in range(1, GROUP):
        added = added + st_x[i]
        largest = jnp.maximum(largest, st_x[i])
    st_y[y] = jnp.where(lane8 == r, jnp.where(sub8 == 0, added, largest), 0.0)
    y_copies = stage(st_y, y, GROUP - 1, [y_peer(o) for o in range(1, y_size)])

    vel_copy.wait_recv()
    mine, other = vel_own[...], vel_got[...]
    cond = jnp.where(g == 0, mine, other)
    uncond = jnp.where(g == 0, other, mine)
    guided = uncond + GUIDANCE * (cond - uncond)
    half = lat_b.shape[1]
    guided = jnp.where(g == 0, guided[:, :half], guided[:, half : 2 * half])
    step = jnp.sum(jnp.where(lane == r, delta_b[...], 0.0), axis=1, keepdims=True)
    new_latents[...] = lat_b[...] + step * guided

    for c in y_copies:
        c.wait_recv()
    added = st_y[0]
    for i in range(1, y_size):
        added = added + st_y[i]
    st_z[z] = added
    z_copies = stage(
        st_z, z, GROUP - 1 + y_size - 1, [z_peer(o) for o in range(1, z_size)]
    )
    for n in range(width // chunk):
        out_copy(n).wait()
    for h in range(HPD):
        for i in range(3):
            for o in ORDER:
                exchange(i, h, o).wait_send()
        for o in ORDER:
            give_back(h, o).wait_send()
    for c in weight_sends + x_copies + y_copies + [vel_copy]:
        c.wait_send()
    for c in z_copies:
        c.wait_recv()
    added = st_z[0]
    for i in range(1, z_size):
        added = added + st_z[i]
    count = GROUP * BLOCK * width
    rms_out[...] = jnp.sqrt(added[0:1, :reqs] / count + 1e-06)
    peak_out[...] = added[1:2, :reqs]
    for c in z_copies:
        c.wait_send()


def solution(mesh, y_size=4, chunk=512):
    reqs = mesh.shape["seq"] // GROUP

    def on_device(
        hidden,
        query_rows,
        key_rows,
        value_rows,
        text_lengths,
        q_gain,
        k_gain,
        o_weight,
        layer_gate,
        final_shift,
        final_scale,
        final_weight,
        final_bias,
        latents,
        step_delta,
    ):
        width = hidden.shape[2]
        heads = GROUP * HPD
        channels = final_weight.shape[1]
        z_size = reqs // y_size
        rows8 = min(8, reqs)
        bf16, f32 = jnp.bfloat16, jnp.float32
        vmem = pltpu.VMEM
        dma = pltpu.SemaphoreType.DMA
        stats = GROUP - 1 + y_size - 1 + z_size - 1
        any_spec = pl.BlockSpec(memory_space=pl.ANY)
        vmem_spec = pl.BlockSpec(memory_space=pltpu.VMEM)
        sds = jax.ShapeDtypeStruct
        return pl.pallas_call(
            functools.partial(kernel, reqs, y_size, chunk),
            out_shape=(
                sds(latents.shape, f32),
                sds(hidden.shape, bf16),
                sds((1, reqs), f32),
                sds((1, reqs), f32),
            ),
            in_specs=[any_spec] * 15,
            out_specs=(vmem_spec, any_spec, vmem_spec, vmem_spec),
            scratch_shapes=[
                vmem((HPD, GROUP, BLOCK, HD), bf16),
                vmem((HPD, GROUP, BLOCK, HD), bf16),
                vmem((HPD, GROUP, BLOCK, HD), bf16),
                vmem((HPD, GROUP, BLOCK, HD), bf16),
                vmem((heads, BLOCK, HD), bf16),
                vmem((heads * HD, width), bf16),
                vmem((BLOCK, width), bf16),
                vmem((BLOCK, width), bf16),
                vmem((BLOCK, width), f32),
                vmem((rows8, width), f32),
                vmem((rows8, width), f32),
                vmem((rows8, width), f32),
                vmem((width, channels), bf16),
                vmem((1, channels), f32),
                vmem(latents.shape, f32),
                vmem((1, reqs), jnp.int32),
                vmem((1, reqs), f32),
                vmem((1, HD), f32),
                vmem((1, HD), f32),
                vmem((IMG_DEV, 128), f32),
                vmem((IMG_DEV, 128), f32),
                vmem((GROUP, 8, 128), f32),
                vmem((y_size, 8, 128), f32),
                vmem((z_size, 8, 128), f32),
                dma((3, HPD, GROUP - 1)),
                dma((3, HPD, GROUP - 1)),
                dma((3, HPD)),
                dma((HPD, GROUP - 1)),
                dma((HPD, GROUP - 1)),
                dma((4,)),
                dma((4,)),
                dma((4,)),
                dma((11,)),
                dma((width // chunk,)),
                dma((2,)),
                dma((stats,)),
                dma((stats,)),
            ],
            compiler_params=pltpu.CompilerParams(
                collective_id=0, has_side_effects=True, vmem_limit_bytes=56 * 1024 * 1024
            ),
        )(
            hidden,
            query_rows,
            key_rows,
            value_rows,
            text_lengths,
            q_gain.reshape(1, -1),
            k_gain.reshape(1, -1),
            o_weight,
            layer_gate,
            final_shift,
            final_scale,
            final_weight,
            final_bias.reshape(1, -1),
            latents,
            step_delta.reshape(1, -1),
        )

    return jax.shard_map(
        on_device,
        mesh=mesh,
        in_specs=(
            P("guide", "seq", None),
            P("guide", "seq", None),
            P("guide", "seq", None),
            P("guide", "seq", None),
            P("guide", None),
            P(),
            P(),
            P("guide", None),
            P("guide", None, None),
            P("guide", None, None),
            P("guide", None, None),
            P(),
            P(),
            P("seq", "guide"),
            P(),
        ),
        out_specs=(P("seq", "guide"), P("guide", "seq", None), P("guide", None), P("guide", None)),
        check_vma=False,
    )
```

```python
import functools
import math

import jax
import jax.numpy as jnp
from jax import lax
from jax.experimental import pallas as pl
from jax.experimental.pallas import tpu as pltpu
from jax.sharding import PartitionSpec as P

HD = 128
GROUP = 4
TXT_DEV = 128
IMG_DEV = 64
BLOCK = TXT_DEV + IMG_DEV
HPD = 3
GUIDANCE = 3.5
ORDER = (2, 1, 3)


def normalize(rows, gain, factor):
    values = rows.astype(jnp.float32)
    inv = lax.rsqrt(jnp.mean(values * values, axis=-1, keepdims=True) + 1e-06)
    return (values * inv * gain * factor).astype(jnp.bfloat16)


def kernel(
    reqs,
    y_size,
    chunk,
    hidden,
    query,
    key,
    value,
    lengths,
    q_gain,
    k_gain,
    o_weight,
    gate,
    shift,
    scale,
    f_weight,
    f_bias,
    latents,
    delta,
    new_latents,
    hidden_out,
    rms_out,
    peak_out,
    qb,
    kb,
    vb,
    ob,
    att,
    wb,
    hid,
    part,
    gate_b,
    shift_b,
    scale_b,
    fw_b,
    bias_b,
    lat_b,
    len_b,
    delta_b,
    qg_b,
    kg_b,
    vel_own,
    vel_got,
    st_p,
    st_z,
    in_send,
    in_recv,
    in_local,
    o_send,
    o_recv,
    w_send,
    w_recv,
    w_local,
    loc,
    v_sem,
    s_send,
    s_recv,
):
    z_size = reqs // y_size
    width = hidden.shape[2]
    heads = GROUP * HPD
    g = lax.axis_index("guide")
    s = lax.axis_index("seq")
    x = s // reqs
    r = s % reqs
    y = r % y_size
    z = r // y_size

    def seq_of(xx, zz, yy):
        return xx * reqs + zz * y_size + yy

    def x_peer(o):
        return lax.rem(x + o, GROUP)

    def z_peer(o):
        return seq_of(x, lax.rem(z + o, z_size), y)

    plane = [(i, j) for i in range(GROUP) for j in range(y_size) if i + j > 0]
    plane = [seq_of(x_peer(i), z, lax.rem(y + j, y_size)) for i, j in plane]
    z_peers = [z_peer(o) for o in range(1, z_size)]
    barrier = pltpu.get_barrier_semaphore()
    pl.semaphore_signal(barrier, inc=1, device_id={"guide": 1 - g})
    for peer in plane + z_peers:
        pl.semaphore_signal(barrier, inc=1, device_id={"seq": peer})

    tensors = ((key, kb), (value, vb), (query, qb))

    def columns(owner, h):
        return pl.ds(pl.multiple_of((owner * HPD + h) * HD, HD), HD)

    own = []
    for h in range(HPD):
        row = []
        for i, (src, dst) in enumerate(tensors):
            c = pltpu.make_async_copy(
                src.at[0, :, columns(x, h)], dst.at[h, x], in_local.at[i, h]
            )
            c.start()
            row.append(c)
        own.append(row)
    group8 = pl.ds(pl.multiple_of((r // 8) * 8, 8), 8) if reqs >= 8 else pl.ds(0, reqs)
    row8 = r % 8
    small = [
        (q_gain, qg_b),
        (k_gain, kg_b),
        (lengths, len_b),
        (gate.at[0, group8], gate_b),
        (hidden.at[0], hid),
        (shift.at[0, group8], shift_b),
        (scale.at[0, group8], scale_b),
        (f_weight, fw_b),
        (f_bias, bias_b),
        (latents, lat_b),
        (delta, delta_b),
    ]
    small = [pltpu.make_async_copy(a, b, loc.at[i]) for i, (a, b) in enumerate(small)]
    for c in small:
        c.start()

    pl.semaphore_wait(barrier, len(plane) + len(z_peers) + 1)

    def exchange(i, h, o):
        src, dst = tensors[i]
        t = x_peer(o)
        return pltpu.make_async_remote_copy(
            src_ref=src.at[0, :, columns(t, h)],
            dst_ref=dst.at[h, x],
            send_sem=in_send.at[i, h, o - 1],
            recv_sem=in_recv.at[i, h, o - 1],
            device_id={"seq": seq_of(t, z, y)},
        )

    for h in range(HPD):
        for i in range(3):
            for o in ORDER:
                exchange(i, h, o).start()

    def weight_pieces():
        first = (HPD - 1) * HD
        pieces = []
        for p in range(GROUP // 2):
            owner = g * (GROUP // 2) + p
            pieces.append((pl.ds(p * HPD * HD, first), pl.ds(pl.multiple_of(owner * first, HD), first)))
            pieces.append(
                (
                    pl.ds(p * HPD * HD + first, HD),
                    pl.ds(pl.multiple_of(GROUP * first + owner * HD, HD), HD),
                )
            )
        return pieces

    weight_sends, weight_locals = [], []
    for i, (a, b) in enumerate(weight_pieces()):
        c = pltpu.make_async_remote_copy(
            src_ref=o_weight.at[a],
            dst_ref=wb.at[b],
            send_sem=w_send.at[i],
            recv_sem=w_recv.at[i],
            device_id={"guide": 1 - g},
        )
        c.start()
        weight_sends.append(c)
        c = pltpu.make_async_copy(o_weight.at[a], wb.at[b], w_local.at[i])
        c.start()
        weight_locals.append(c)

    def give_back(h, o):
        t = x_peer(o)
        return pltpu.make_async_remote_copy(
            src_ref=ob.at[h, t],
            dst_ref=att.at[x * HPD + h],
            send_sem=o_send.at[h, o - 1],
            recv_sem=o_recv.at[h, o - 1],
            device_id={"seq": seq_of(t, z, y)},
        )

    for c in small[:3]:
        c.wait()
    lane = lax.broadcasted_iota(jnp.int32, (1, len_b.shape[1]), 1)
    length = jnp.sum(jnp.where(lane == r, len_b[...], 0), axis=1, keepdims=True)
    position = lax.broadcasted_iota(jnp.int32, (1, GROUP * BLOCK), 1)
    within = position % BLOCK
    usable = (within >= TXT_DEV) | ((position // BLOCK) * TXT_DEV + within < length)
    bias = jnp.where(usable, 0.0, -1e30).astype(jnp.float32)
    q_gain_row = qg_b[...]
    k_gain_row = kg_b[...]
    ones = jnp.ones((GROUP * BLOCK, HD), jnp.bfloat16)

    for h in range(HPD):
        for i in range(3):
            own[h][i].wait()
            for o in ORDER:
                exchange(i, h, o).wait_recv()
        keys = normalize(kb[h].reshape(GROUP * BLOCK, HD), k_gain_row, 1.0)
        values = jnp.concatenate([vb[h].reshape(GROUP * BLOCK, HD), ones], axis=1)
        for o in ORDER + (0,):
            t = x_peer(o)
            queries = normalize(qb[h, t], q_gain_row, 1.0 / math.sqrt(HD))
            scores = lax.dot_general(
                queries, keys, (((1,), (1,)), ((), ())), preferred_element_type=jnp.float32
            )
            scores = scores + bias
            top = jnp.max(scores, axis=1, keepdims=True)
            weights = jnp.exp(scores - top).astype(jnp.bfloat16)
            both = jnp.dot(weights, values, preferred_element_type=jnp.float32)
            result = (both[:, :HD] / both[:, HD:]).astype(jnp.bfloat16)
            if o == 0:
                att[x * HPD + h] = result
            else:
                ob[h, t] = result
                give_back(h, o).start()

    for c in weight_locals:
        c.wait()
    for c in weight_sends:
        c.wait_recv()
    for h in range(HPD - 1):
        for o in ORDER:
            give_back(h, o).wait_recv()
    depth = GROUP * (HPD - 1) * HD
    first = jnp.concatenate(
        [att[p * HPD + h] for p in range(GROUP) for h in range(HPD - 1)], axis=1
    )

    def first_part(n, carry):
        cols = pl.ds(pl.multiple_of(n * chunk, chunk), chunk)
        part[:, cols] = jnp.dot(first, wb[:depth, cols], preferred_element_type=jnp.float32)
        return carry

    lax.fori_loop(0, width // chunk, first_part, 0)

    for c in small[3:]:
        c.wait()
    for o in ORDER:
        give_back(HPD - 1, o).wait_recv()
    last = jnp.concatenate([att[p * HPD + HPD - 1] for p in range(GROUP)], axis=1)

    def last_part(n, carry):
        squares, peaks, sums = carry
        cols = pl.ds(pl.multiple_of(n * chunk, chunk), chunk)
        projected = part[:, cols] + jnp.dot(
            last, wb[depth:, cols], preferred_element_type=jnp.float32
        )
        new = (hid[:, cols].astype(jnp.float32) + gate_b[pl.ds(row8, 1), cols] * projected).astype(
            jnp.bfloat16
        )
        hidden_out[0, :, cols] = new
        wide = new.astype(jnp.float32)
        folded = wide.reshape(BLOCK // 8, 8, chunk)
        squares = squares + jnp.sum(folded * folded, axis=0)
        peaks = jnp.maximum(peaks, jnp.max(jnp.abs(folded), axis=0))
        part_sums = wide[TXT_DEV:]
        part[TXT_DEV:, cols] = part_sums
        for k in range(chunk // 128):
            sums = sums + part_sums[:, k * 128 : (k + 1) * 128]
        return squares, peaks, sums

    zero = jnp.zeros((8, chunk), jnp.float32)
    squares, peaks, sums = lax.fori_loop(
        0, width // chunk, last_part, (zero, zero, jnp.zeros((IMG_DEV, 128), jnp.float32))
    )

    total = jnp.sum(jnp.sum(squares, axis=1, keepdims=True), axis=0, keepdims=True)
    peak = jnp.max(jnp.max(peaks, axis=1, keepdims=True), axis=0, keepdims=True)
    sub8 = lax.broadcasted_iota(jnp.int32, (8, 128), 0)
    lane8 = lax.broadcasted_iota(jnp.int32, (8, 128), 1)

    def stage(ref, slot, base, peers):
        copies = []
        for i, peer in enumerate(peers):
            c = pltpu.make_async_remote_copy(
                src_ref=ref.at[slot],
                dst_ref=ref.at[slot],
                send_sem=s_send.at[base + i],
                recv_sem=s_recv.at[base + i],
                device_id={"seq": peer},
            )
            c.start()
            copies.append(c)
        return copies

    here = x * y_size + y
    st_p[here] = jnp.where(lane8 == r, jnp.where(sub8 == 0, total, peak), 0.0)
    p_copies = stage(st_p, here, 0, plane)

    mean = jnp.sum(sums, axis=1, keepdims=True) * (1.0 / width)

    def variance(n, acc):
        cols = pl.ds(pl.multiple_of(n * chunk, chunk), chunk)
        centered = part[TXT_DEV:, cols] - mean
        centered = centered * centered
        for k in range(chunk // 128):
            acc = acc + centered[:, k * 128 : (k + 1) * 128]
        return acc

    var = lax.fori_loop(0, width // chunk, variance, jnp.zeros((IMG_DEV, 128), jnp.float32))
    inv = lax.rsqrt(jnp.sum(var, axis=1, keepdims=True) * (1.0 / width) + 1e-06)

    def velocity_part(n, acc):
        cols = pl.ds(pl.multiple_of(n * chunk, chunk), chunk)
        normed = (part[TXT_DEV:, cols] - mean) * inv
        mod = (
            normed * (1.0 + scale_b[pl.ds(row8, 1), cols]) + shift_b[pl.ds(row8, 1), cols]
        ).astype(jnp.bfloat16)
        return acc + lax.dot_general(
            mod, fw_b[:, cols], (((1,), (1,)), ((), ())), preferred_element_type=jnp.float32
        )

    channels = fw_b.shape[0]
    velocity = lax.fori_loop(
        0, width // chunk, velocity_part, jnp.zeros((IMG_DEV, channels), jnp.float32)
    )
    velocity = velocity + bias_b[...]
    vel_own[...] = jnp.concatenate(
        [velocity, jnp.zeros((IMG_DEV, 128 - channels), jnp.float32)], axis=1
    )
    vel_copy = pltpu.make_async_remote_copy(
        src_ref=vel_own,
        dst_ref=vel_got,
        send_sem=v_sem.at[0],
        recv_sem=v_sem.at[1],
        device_id={"guide": 1 - g},
    )
    vel_copy.start()

    for c in p_copies:
        c.wait_recv()
    added, largest = st_p[0], st_p[0]
    for i in range(1, GROUP * y_size):
        added = added + st_p[i]
        largest = jnp.maximum(largest, st_p[i])
    st_z[z] = jnp.where(sub8 == 0, added, largest)
    z_copies = stage(st_z, z, len(plane), z_peers)

    vel_copy.wait_recv()
    mine, other = vel_own[...], vel_got[...]
    cond = jnp.where(g == 0, mine, other)
    uncond = jnp.where(g == 0, other, mine)
    guided = uncond + GUIDANCE * (cond - uncond)
    half = lat_b.shape[0]
    guided = guided.T
    guided = jnp.where(g == 0, guided[:half], guided[half : 2 * half])
    step = jnp.sum(jnp.where(lane == r, delta_b[...], 0.0), axis=1, keepdims=True)
    new_latents[...] = lat_b[...] + step * guided

    for h in range(HPD):
        for i in range(3):
            for o in ORDER:
                exchange(i, h, o).wait_send()
        for o in ORDER:
            give_back(h, o).wait_send()
    for c in weight_sends + p_copies + [vel_copy]:
        c.wait_send()
    for c in z_copies:
        c.wait_recv()
    added = st_z[0]
    for i in range(1, z_size):
        added = added + st_z[i]
    count = GROUP * BLOCK * width
    rms_out[...] = jnp.sqrt(added[0:1, :reqs] / count + 1e-06)
    peak_out[...] = added[1:2, :reqs]
    for c in z_copies:
        c.wait_send()


def write_out(latents, hidden, rms, peak, latents_out, hidden_out, rms_out, peak_out, sems):
    pairs = ((hidden, hidden_out), (latents, latents_out), (rms, rms_out), (peak, peak_out))
    copies = [pltpu.make_async_copy(a, b, sems.at[i]) for i, (a, b) in enumerate(pairs)]
    for c in copies:
        c.start()
    for c in copies:
        c.wait()


def solution(mesh, y_size=4, chunk=3072):
    reqs = mesh.shape["seq"] // GROUP

    def on_device(
        hidden,
        query_rows,
        key_rows,
        value_rows,
        text_lengths,
        q_gain,
        k_gain,
        o_weight,
        layer_gate,
        final_shift,
        final_scale,
        final_weight,
        final_bias,
        latents,
        step_delta,
    ):
        width = hidden.shape[2]
        heads = GROUP * HPD
        channels = final_weight.shape[1]
        z_size = reqs // y_size
        rows8 = min(8, reqs)
        bf16, f32 = jnp.bfloat16, jnp.float32
        vmem = pltpu.VMEM
        dma = pltpu.SemaphoreType.DMA
        stats = GROUP * y_size - 1 + z_size - 1
        any_spec = pl.BlockSpec(memory_space=pltpu.HBM)
        vmem_spec = pl.BlockSpec(memory_space=pltpu.VMEM)
        sds = jax.ShapeDtypeStruct
        results = (
            sds(latents.shape[::-1], f32),
            sds(hidden.shape, bf16),
            sds((1, reqs), f32),
            sds((1, reqs), f32),
        )
        new, out, rms, peak = pl.pallas_call(
            functools.partial(kernel, reqs, y_size, chunk),
            out_shape=tuple(vmem(v.shape, v.dtype) for v in results),
            in_specs=[any_spec] * 15,
            out_specs=(vmem_spec,) * 4,
            scratch_shapes=[
                vmem((HPD, GROUP, BLOCK, HD), bf16),
                vmem((HPD, GROUP, BLOCK, HD), bf16),
                vmem((HPD, GROUP, BLOCK, HD), bf16),
                vmem((HPD, GROUP, BLOCK, HD), bf16),
                vmem((heads, BLOCK, HD), bf16),
                vmem((heads * HD, width), bf16),
                vmem((BLOCK, width), bf16),
                vmem((BLOCK, width), f32),
                vmem((rows8, width), f32),
                vmem((rows8, width), f32),
                vmem((rows8, width), f32),
                vmem((channels, width), bf16),
                vmem((1, channels), f32),
                vmem(latents.shape[::-1], f32),
                vmem((1, reqs), jnp.int32),
                vmem((1, reqs), f32),
                vmem((1, HD), f32),
                vmem((1, HD), f32),
                vmem((IMG_DEV, 128), f32),
                vmem((IMG_DEV, 128), f32),
                vmem((GROUP * y_size, 8, 128), f32),
                vmem((z_size, 8, 128), f32),
                dma((3, HPD, GROUP - 1)),
                dma((3, HPD, GROUP - 1)),
                dma((3, HPD)),
                dma((HPD, GROUP - 1)),
                dma((HPD, GROUP - 1)),
                dma((4,)),
                dma((4,)),
                dma((4,)),
                dma((11,)),
                dma((2,)),
                dma((stats,)),
                dma((stats,)),
            ],
            compiler_params=pltpu.CompilerParams(
                collective_id=0, has_side_effects=True, vmem_limit_bytes=48 * 1024 * 1024
            ),
        )(
            *(
                pltpu.with_memory_space_constraint(v, pltpu.HBM)
                for v in (
                    hidden,
                    query_rows,
                    key_rows,
                    value_rows,
                    text_lengths,
                    q_gain.reshape(1, -1),
                    k_gain.reshape(1, -1),
                    o_weight,
                    layer_gate,
                    final_shift,
                    final_scale,
                    final_weight.T,
                    final_bias.reshape(1, -1),
                    latents.T,
                    step_delta.reshape(1, -1),
                )
            )
        )
        new, out, rms, peak = pl.pallas_call(
            write_out,
            out_shape=tuple(pltpu.HBM(v.shape, v.dtype) for v in results),
            in_specs=[vmem_spec] * 4,
            out_specs=[any_spec] * 4,
            scratch_shapes=[dma((4,))],
        )(*(pltpu.with_memory_space_constraint(v, pltpu.VMEM) for v in (new, out, rms, peak)))
        return new.T, out, rms, peak

    return jax.shard_map(
        on_device,
        mesh=mesh,
        in_specs=(
            P("guide", "seq", None),
            P("guide", "seq", None),
            P("guide", "seq", None),
            P("guide", "seq", None),
            P("guide", None),
            P(),
            P(),
            P("guide", None),
            P("guide", None, None),
            P("guide", None, None),
            P("guide", None, None),
            P(),
            P(),
            P("seq", "guide"),
            P(),
        ),
        out_specs=(P("seq", "guide"), P("guide", "seq", None), P("guide", None), P("guide", None)),
        check_vma=False,
    )
```

```python
import functools
import math

import jax
import jax.numpy as jnp
from jax import lax
from jax.experimental import pallas as pl
from jax.experimental.pallas import tpu as pltpu
from jax.sharding import PartitionSpec as P

HD = 128
GROUP = 4
TXT_DEV = 128
IMG_DEV = 64
BLOCK = TXT_DEV + IMG_DEV
HPD = 3
GUIDANCE = 3.5
ORDER = (2, 1, 3)


def normalize(rows, gain, factor):
    values = rows.astype(jnp.float32)
    inv = lax.rsqrt(jnp.mean(values * values, axis=-1, keepdims=True) + 1e-06)
    return (values * inv * gain * factor).astype(jnp.bfloat16)


def kernel(
    reqs,
    y_size,
    chunk,
    hidden,
    query,
    key,
    value,
    lengths,
    q_gain,
    k_gain,
    o_weight,
    gate,
    shift,
    scale,
    f_weight,
    f_bias,
    latents,
    delta,
    new_latents,
    hidden_out,
    rms_out,
    peak_out,
    qb,
    kb,
    vb,
    ob,
    att,
    wb,
    hid,
    part,
    gate_b,
    shift_b,
    scale_b,
    fw_b,
    bias_b,
    lat_b,
    len_b,
    delta_b,
    qg_b,
    kg_b,
    vel_own,
    vel_got,
    st_p,
    st_z,
    in_send,
    in_recv,
    in_local,
    o_send,
    o_recv,
    w_send,
    w_recv,
    w_local,
    loc,
    v_sem,
    s_send,
    s_recv,
):
    z_size = reqs // y_size
    width = hidden.shape[2]
    heads = GROUP * HPD
    g = lax.axis_index("guide")
    s = lax.axis_index("seq")
    x = s // reqs
    r = s % reqs
    y = r % y_size
    z = r // y_size

    def seq_of(xx, zz, yy):
        return xx * reqs + zz * y_size + yy

    def x_peer(o):
        return lax.rem(x + o, GROUP)

    def z_peer(o):
        return seq_of(x, lax.rem(z + o, z_size), y)

    plane = [(i, j) for i in range(GROUP) for j in range(y_size) if i + j > 0]
    plane.sort(key=lambda p: -min(p[0], GROUP - p[0]) - min(p[1], y_size - p[1]))
    plane = [seq_of(x_peer(i), z, lax.rem(y + j, y_size)) for i, j in plane]
    z_peers = [z_peer(o) for o in sorted(range(1, z_size), key=lambda o: -min(o, z_size - o))]
    barrier = pltpu.get_barrier_semaphore()
    pl.semaphore_signal(barrier, inc=1, device_id={"guide": 1 - g})
    for peer in plane + z_peers:
        pl.semaphore_signal(barrier, inc=1, device_id={"seq": peer})

    tensors = ((key, kb), (value, vb), (query, qb))

    def columns(owner, h):
        return pl.ds(pl.multiple_of((owner * HPD + h) * HD, HD), HD)

    own = []
    for h in range(HPD):
        row = []
        for i, (src, dst) in enumerate(tensors):
            c = pltpu.make_async_copy(
                src.at[0, :, columns(x, h)], dst.at[h, x], in_local.at[i, h]
            )
            c.start()
            row.append(c)
        own.append(row)
    group8 = pl.ds(pl.multiple_of((r // 8) * 8, 8), 8) if reqs >= 8 else pl.ds(0, reqs)
    row8 = r % 8
    small = [
        (q_gain, qg_b),
        (k_gain, kg_b),
        (lengths, len_b),
        (gate.at[0, group8], gate_b),
        (hidden.at[0], hid),
        (shift.at[0, group8], shift_b),
        (scale.at[0, group8], scale_b),
        (f_weight, fw_b),
        (f_bias, bias_b),
        (latents, lat_b),
        (delta, delta_b),
    ]
    small = [pltpu.make_async_copy(a, b, loc.at[i]) for i, (a, b) in enumerate(small)]
    for c in small:
        c.start()

    pl.semaphore_wait(barrier, len(plane) + len(z_peers) + 1)

    def exchange(i, h, o):
        src, dst = tensors[i]
        t = x_peer(o)
        return pltpu.make_async_remote_copy(
            src_ref=src.at[0, :, columns(t, h)],
            dst_ref=dst.at[h, x],
            send_sem=in_send.at[i, h, o - 1],
            recv_sem=in_recv.at[i, h, o - 1],
            device_id={"seq": seq_of(t, z, y)},
        )

    pieces = [(i, h, o) for h in range(HPD) for i in range(3) for o in ORDER]
    now = 11

    def send(some):
        for i, h, o in some:
            exchange(i, h, o).start()

    send(pieces[:now])

    @pl.when(g == 0)
    def _():
        send(pieces[now:])

    def weight_pieces():
        first = (HPD - 1) * HD
        pieces = []
        for p in range(GROUP // 2):
            owner = g * (GROUP // 2) + p
            pieces.append((pl.ds(p * HPD * HD, first), pl.ds(pl.multiple_of(owner * first, HD), first)))
            pieces.append(
                (
                    pl.ds(p * HPD * HD + first, HD),
                    pl.ds(pl.multiple_of(GROUP * first + owner * HD, HD), HD),
                )
            )
        return pieces

    weight_sends, weight_locals = [], []
    for i, (a, b) in enumerate(weight_pieces()):
        c = pltpu.make_async_remote_copy(
            src_ref=o_weight.at[a],
            dst_ref=wb.at[b],
            send_sem=w_send.at[i],
            recv_sem=w_recv.at[i],
            device_id={"guide": 1 - g},
        )
        c.start()
        weight_sends.append(c)
        c = pltpu.make_async_copy(o_weight.at[a], wb.at[b], w_local.at[i])
        c.start()
        weight_locals.append(c)

    def give_back(h, o):
        t = x_peer(o)
        return pltpu.make_async_remote_copy(
            src_ref=ob.at[h, t],
            dst_ref=att.at[x * HPD + h],
            send_sem=o_send.at[h, o - 1],
            recv_sem=o_recv.at[h, o - 1],
            device_id={"seq": seq_of(t, z, y)},
        )

    for c in small[:3]:
        c.wait()
    lane = lax.broadcasted_iota(jnp.int32, (1, len_b.shape[1]), 1)
    length = jnp.sum(jnp.where(lane == r, len_b[...], 0), axis=1, keepdims=True)
    position = lax.broadcasted_iota(jnp.int32, (1, GROUP * BLOCK), 1)
    within = position % BLOCK
    usable = (within >= TXT_DEV) | ((position // BLOCK) * TXT_DEV + within < length)
    bias = jnp.where(usable, 0.0, -1e30).astype(jnp.float32)
    q_gain_row = qg_b[...]
    k_gain_row = kg_b[...]
    ones = jnp.ones((GROUP * BLOCK, HD), jnp.bfloat16)

    for h in range(HPD):
        for i in range(3):
            own[h][i].wait()
            for o in ORDER:
                exchange(i, h, o).wait_recv()
        if h == 0:

            @pl.when(g == 1)
            def _():
                send(pieces[now:])

        keys = normalize(kb[h].reshape(GROUP * BLOCK, HD), k_gain_row, 1.0)
        values = jnp.concatenate([vb[h].reshape(GROUP * BLOCK, HD), ones], axis=1)
        for o in ORDER + (0,):
            t = x_peer(o)
            queries = normalize(qb[h, t], q_gain_row, 1.0 / math.sqrt(HD))
            scores = lax.dot_general(
                queries, keys, (((1,), (1,)), ((), ())), preferred_element_type=jnp.float32
            )
            scores = scores + bias
            top = jnp.max(scores, axis=1, keepdims=True)
            weights = jnp.exp(scores - top).astype(jnp.bfloat16)
            both = jnp.dot(weights, values, preferred_element_type=jnp.float32)
            result = (both[:, :HD] / both[:, HD:]).astype(jnp.bfloat16)
            if o == 0:
                att[x * HPD + h] = result
            else:
                ob[h, t] = result
                give_back(h, o).start()

    for c in weight_locals:
        c.wait()
    for c in weight_sends:
        c.wait_recv()
    for h in range(HPD - 1):
        for o in ORDER:
            give_back(h, o).wait_recv()
    depth = GROUP * (HPD - 1) * HD
    first = jnp.concatenate(
        [att[p * HPD + h] for p in range(GROUP) for h in range(HPD - 1)], axis=1
    )

    def first_part(n, carry):
        cols = pl.ds(pl.multiple_of(n * chunk, chunk), chunk)
        part[:, cols] = jnp.dot(first, wb[:depth, cols], preferred_element_type=jnp.float32)
        return carry

    lax.fori_loop(0, width // chunk, first_part, 0)

    for c in small[3:]:
        c.wait()
    for o in ORDER:
        give_back(HPD - 1, o).wait_recv()
    last = jnp.concatenate([att[p * HPD + HPD - 1] for p in range(GROUP)], axis=1)

    def last_part(n, carry):
        squares, peaks, sums = carry
        cols = pl.ds(pl.multiple_of(n * chunk, chunk), chunk)
        projected = part[:, cols] + jnp.dot(
            last, wb[depth:, cols], preferred_element_type=jnp.float32
        )
        new = (hid[:, cols].astype(jnp.float32) + gate_b[pl.ds(row8, 1), cols] * projected).astype(
            jnp.bfloat16
        )
        hidden_out[0, :, cols] = new
        wide = new.astype(jnp.float32)
        folded = wide.reshape(BLOCK // 8, 8, chunk)
        squares = squares + jnp.sum(folded * folded, axis=0)
        peaks = jnp.maximum(peaks, jnp.max(jnp.abs(folded), axis=0))
        part_sums = wide[TXT_DEV:]
        part[TXT_DEV:, cols] = part_sums
        for k in range(chunk // 128):
            sums = sums + part_sums[:, k * 128 : (k + 1) * 128]
        return squares, peaks, sums

    zero = jnp.zeros((8, chunk), jnp.float32)
    squares, peaks, sums = lax.fori_loop(
        0, width // chunk, last_part, (zero, zero, jnp.zeros((IMG_DEV, 128), jnp.float32))
    )

    total = jnp.sum(jnp.sum(squares, axis=1, keepdims=True), axis=0, keepdims=True)
    peak = jnp.max(jnp.max(peaks, axis=1, keepdims=True), axis=0, keepdims=True)
    lanes = lax.broadcasted_iota(jnp.int32, (1, 128), 1)

    def stage(ref, slot, base, peers):
        copies = []
        for i, peer in enumerate(peers):
            c = pltpu.make_async_remote_copy(
                src_ref=ref.at[slot],
                dst_ref=ref.at[slot],
                send_sem=s_send.at[base + i],
                recv_sem=s_recv.at[base + i],
                device_id={"seq": peer},
            )
            c.start()
            copies.append(c)
        return copies

    here = x * y_size + y
    st_p[here] = jnp.where(lanes == r, total, jnp.where(lanes == 64 + r, peak, 0.0))
    p_copies = stage(st_p, here, 0, plane)

    mean = jnp.sum(sums, axis=1, keepdims=True) * (1.0 / width)

    def variance(n, acc):
        cols = pl.ds(pl.multiple_of(n * chunk, chunk), chunk)
        centered = part[TXT_DEV:, cols] - mean
        centered = centered * centered
        for k in range(chunk // 128):
            acc = acc + centered[:, k * 128 : (k + 1) * 128]
        return acc

    var = lax.fori_loop(0, width // chunk, variance, jnp.zeros((IMG_DEV, 128), jnp.float32))
    inv = lax.rsqrt(jnp.sum(var, axis=1, keepdims=True) * (1.0 / width) + 1e-06)

    def velocity_part(n, acc):
        cols = pl.ds(pl.multiple_of(n * chunk, chunk), chunk)
        normed = (part[TXT_DEV:, cols] - mean) * inv
        mod = (
            normed * (1.0 + scale_b[pl.ds(row8, 1), cols]) + shift_b[pl.ds(row8, 1), cols]
        ).astype(jnp.bfloat16)
        return acc + lax.dot_general(
            mod, fw_b[:, cols], (((1,), (1,)), ((), ())), preferred_element_type=jnp.float32
        )

    channels = fw_b.shape[0]
    velocity = lax.fori_loop(
        0, width // chunk, velocity_part, jnp.zeros((IMG_DEV, channels), jnp.float32)
    )
    velocity = velocity + bias_b[...]
    vel_own[...] = jnp.concatenate(
        [velocity, jnp.zeros((IMG_DEV, 128 - channels), jnp.float32)], axis=1
    )
    vel_copy = pltpu.make_async_remote_copy(
        src_ref=vel_own,
        dst_ref=vel_got,
        send_sem=v_sem.at[0],
        recv_sem=v_sem.at[1],
        device_id={"guide": 1 - g},
    )
    vel_copy.start()

    for c in p_copies:
        c.wait_recv()
    added, largest = st_p[0], st_p[0]
    for i in range(1, GROUP * y_size):
        added = added + st_p[i]
        largest = jnp.maximum(largest, st_p[i])
    st_z[z] = jnp.where(lanes < 64, added, largest)
    z_copies = stage(st_z, z, len(plane), z_peers)

    vel_copy.wait_recv()
    mine, other = vel_own[...], vel_got[...]
    cond = jnp.where(g == 0, mine, other)
    uncond = jnp.where(g == 0, other, mine)
    guided = uncond + GUIDANCE * (cond - uncond)
    half = lat_b.shape[0]
    guided = guided.T
    guided = jnp.where(g == 0, guided[:half], guided[half : 2 * half])
    step = jnp.sum(jnp.where(lane == r, delta_b[...], 0.0), axis=1, keepdims=True)
    new_latents[...] = lat_b[...] + step * guided

    for h in range(HPD):
        for i in range(3):
            for o in ORDER:
                exchange(i, h, o).wait_send()
        for o in ORDER:
            give_back(h, o).wait_send()
    for c in weight_sends + p_copies + [vel_copy]:
        c.wait_send()
    for c in z_copies:
        c.wait_recv()
    added = st_z[0]
    for i in range(1, z_size):
        added = added + st_z[i]
    count = GROUP * BLOCK * width
    rms_out[...] = jnp.sqrt(added[:, :reqs] / count + 1e-06)
    peak_out[...] = added[:, 64 : 64 + reqs]
    for c in z_copies:
        c.wait_send()


def write_out(latents, hidden, rms, peak, latents_out, hidden_out, rms_out, peak_out, sems):
    pairs = ((hidden, hidden_out), (latents, latents_out), (rms, rms_out), (peak, peak_out))
    copies = [pltpu.make_async_copy(a, b, sems.at[i]) for i, (a, b) in enumerate(pairs)]
    for c in copies:
        c.start()
    for c in copies:
        c.wait()


def solution(mesh, y_size=4, chunk=3072):
    reqs = mesh.shape["seq"] // GROUP

    def on_device(
        hidden,
        query_rows,
        key_rows,
        value_rows,
        text_lengths,
        q_gain,
        k_gain,
        o_weight,
        layer_gate,
        final_shift,
        final_scale,
        final_weight,
        final_bias,
        latents,
        step_delta,
    ):
        width = hidden.shape[2]
        heads = GROUP * HPD
        channels = final_weight.shape[1]
        z_size = reqs // y_size
        rows8 = min(8, reqs)
        bf16, f32 = jnp.bfloat16, jnp.float32
        vmem = pltpu.VMEM
        dma = pltpu.SemaphoreType.DMA
        stats = GROUP * y_size - 1 + z_size - 1
        any_spec = pl.BlockSpec(memory_space=pltpu.HBM)
        vmem_spec = pl.BlockSpec(memory_space=pltpu.VMEM)
        sds = jax.ShapeDtypeStruct
        results = (
            sds(latents.shape[::-1], f32),
            sds(hidden.shape, bf16),
            sds((1, reqs), f32),
            sds((1, reqs), f32),
        )
        new, out, rms, peak = pl.pallas_call(
            functools.partial(kernel, reqs, y_size, chunk),
            out_shape=tuple(vmem(v.shape, v.dtype) for v in results),
            in_specs=[any_spec] * 15,
            out_specs=(vmem_spec,) * 4,
            scratch_shapes=[
                vmem((HPD, GROUP, BLOCK, HD), bf16),
                vmem((HPD, GROUP, BLOCK, HD), bf16),
                vmem((HPD, GROUP, BLOCK, HD), bf16),
                vmem((HPD, GROUP, BLOCK, HD), bf16),
                vmem((heads, BLOCK, HD), bf16),
                vmem((heads * HD, width), bf16),
                vmem((BLOCK, width), bf16),
                vmem((BLOCK, width), f32),
                vmem((rows8, width), f32),
                vmem((rows8, width), f32),
                vmem((rows8, width), f32),
                vmem((channels, width), bf16),
                vmem((1, channels), f32),
                vmem(latents.shape[::-1], f32),
                vmem((1, reqs), jnp.int32),
                vmem((1, reqs), f32),
                vmem((1, HD), f32),
                vmem((1, HD), f32),
                vmem((IMG_DEV, 128), f32),
                vmem((IMG_DEV, 128), f32),
                vmem((GROUP * y_size, 1, 128), f32),
                vmem((z_size, 1, 128), f32),
                dma((3, HPD, GROUP - 1)),
                dma((3, HPD, GROUP - 1)),
                dma((3, HPD)),
                dma((HPD, GROUP - 1)),
                dma((HPD, GROUP - 1)),
                dma((4,)),
                dma((4,)),
                dma((4,)),
                dma((11,)),
                dma((2,)),
                dma((stats,)),
                dma((stats,)),
            ],
            compiler_params=pltpu.CompilerParams(
                collective_id=0, has_side_effects=True, vmem_limit_bytes=48 * 1024 * 1024
            ),
        )(
            *(
                pltpu.with_memory_space_constraint(v, pltpu.HBM)
                for v in (
                    hidden,
                    query_rows,
                    key_rows,
                    value_rows,
                    text_lengths,
                    q_gain.reshape(1, -1),
                    k_gain.reshape(1, -1),
                    o_weight,
                    layer_gate,
                    final_shift,
                    final_scale,
                    final_weight.T,
                    final_bias.reshape(1, -1),
                    latents.T,
                    step_delta.reshape(1, -1),
                )
            )
        )
        new, out, rms, peak = pl.pallas_call(
            write_out,
            out_shape=tuple(pltpu.HBM(v.shape, v.dtype) for v in results),
            in_specs=[vmem_spec] * 4,
            out_specs=[any_spec] * 4,
            scratch_shapes=[dma((4,))],
        )(*(pltpu.with_memory_space_constraint(v, pltpu.VMEM) for v in (new, out, rms, peak)))
        return new.T, out, rms, peak

    return jax.shard_map(
        on_device,
        mesh=mesh,
        in_specs=(
            P("guide", "seq", None),
            P("guide", "seq", None),
            P("guide", "seq", None),
            P("guide", "seq", None),
            P("guide", None),
            P(),
            P(),
            P("guide", None),
            P("guide", None, None),
            P("guide", None, None),
            P("guide", None, None),
            P(),
            P(),
            P("seq", "guide"),
            P(),
        ),
        out_specs=(P("seq", "guide"), P("guide", "seq", None), P("guide", None), P("guide", None)),
        check_vma=False,
    )
```
